128 devices in a mesh: ep: 64 (over y, z, x), tp: 2 (over core).
Axes of the slice: x: 4, y: 4, z: 4, core: 2. Of those that a mesh axis runs over, the one named last changes fastest.
Arguments:
- tokens: bfloat16 [8192, 3584], P('ep'), may hold values from -6 to 6
- expert_ids: int32 [8192, 8], P('ep'), may hold values from 0 to 63, all different within a row; in each aligned block of 128 rows (0 to 127, 128 to 255, ...) at most 24 rows name the same one
- gate_values: float32 [8192, 8], P('ep'), may hold values from 0.05 to 1
- w_gate: bfloat16 [64, 3584, 1024], P('ep', None, 'tp'), may hold values from -0.09375 to 0.09375
- w_up: bfloat16 [64, 3584, 1024], P('ep', None, 'tp'), may hold values from -0.09375 to 0.09375
- w_down: bfloat16 [64, 1024, 3584], P('ep', 'tp'), may hold values from -0.1875 to 0.1875
- shared_gate: bfloat16 [3584, 1024], P(None, 'tp'), may hold values from -0.09375 to 0.09375
- shared_up: bfloat16 [3584, 1024], P(None, 'tp'), may hold values from -0.09375 to 0.09375
- shared_down: bfloat16 [1024, 3584], P('tp'), may hold values from -0.1875 to 0.1875
Outputs:
- layer_out: bfloat16 [8192, 3584], P('ep', 'tp')
The draws below stay inside these ranges and needn't reach their ends.
Inputs may be any that keep to these rules, and one draw needn't show every extreme that they name: `expert_ids`: each row names 8 different experts; within the rows of one index of ep (aligned blocks of 128 rows) no expert is named by more than 24 rows.
All inputs are finite; a program needn't handle non-finite values.
Results may differ from the reference program's by a relative error of at most 0.0085.
Values may be sent and summed in bfloat16 or wider, within the bound.
No kernel may reach another device: no remote copies, remote signals or barrier semaphores. Data moves between devices by JAX's collectives and lax.ppermute only.
A program may use at most 128 MiB of HBM per device.

```python
import math
import jax
import jax.numpy as jnp
import numpy as np
from jax import lax

D = 3584
FE = 1024
FS = 1024
TOPK = 8
TOK_DEV = 128
EXPERTS = 64
TOKENS = 8192
CAP = 24
N_EP = 64


def levels(key, extent, cuts, low, top_value):
    level, own = 1.0, jax.random.fold_in(key, 6)
    for position, shards_of in cuts:
        steps = jnp.exp(jax.random.uniform(jax.random.fold_in(own, position), (shards_of,), jnp.float32, low / len(cuts), top_value / len(cuts)))
        level = level * jnp.repeat(steps, extent[position] // shards_of).reshape([-1 if axis == position else 1 for axis in range(len(extent))])
    return level


def routed_block(key, own, number, rows, count, top, reach, slope):
    order = jax.random.permutation(key, count)
    crowded, ordinary = shares(count, rows * top, reach, slope, True), shares(count, rows * top, reach, slope, False)
    places = jnp.arange(count)

    def named(tallies, turn):
        used = int((tallies > 0).sum())
        fixed = max(1, used // 4)
        shifted = fixed + (places - fixed + turn * (used - fixed)) % max(1, count - fixed)
        return jnp.zeros((count,), jnp.int32).at[order[jnp.where(places < fixed, places, shifted)]].set(jnp.asarray(tallies, jnp.int32))

    tallies = jnp.where(number % 4 == 0, named(crowded, number // 4), named(ordinary, number - number // 4 - 1))
    mixed = jax.random.permutation(jax.random.fold_in(own, 3), count)
    donor, receiver = mixed[0:count // 2 * 2:2], mixed[1:count // 2 * 2:2]
    margin = jnp.minimum(tallies[donor] - 1, reach - tallies[receiver]) // 2
    margin = jnp.where((donor == order[0]) | (receiver == order[0]) | (tallies[receiver] == 0), 0, jnp.maximum(margin, 0))
    shifted = jax.random.randint(jax.random.fold_in(own, 4), (count // 2,), 0, 1 << 20) % (margin + 1)
    tallies = tallies.at[donor].add(-shifted).at[receiver].add(shifted)
    labels = jnp.searchsorted(jnp.cumsum(tallies), jnp.arange(rows * top), side="right").astype(jnp.int32)
    grid = labels.reshape(top, rows).T
    grid = grid[jax.random.permutation(jax.random.fold_in(own, 1), rows)]
    turn = jax.random.randint(jax.random.fold_in(own, 2), (rows, 1), 0, top)
    return jnp.take_along_axis(grid, (jnp.arange(top)[None, :] + turn) % top, axis=1)


def shares(count, total, reach, skew, full):
    weights = [(1 << 20) // math.isqrt(grade ** skew) + 1 for grade in range(1, count + 1)]
    largest = reach if full else min(reach, max(-(-total // count), total * weights[0] // sum(weights)))
    least = 1 if total - largest >= count - 1 else 0
    holding, surplus = [largest] + [least] * (count - 1), total - largest - least * (count - 1)
    while surplus > 0:
        free = [i for i in range(1, count) if holding[i] < largest] or [i for i in range(1, count) if holding[i] < reach]
        whole, budget = sum([weights[i] for i in free]), surplus
        for i in free:
            extra = min(reach - holding[i], max(1, budget * weights[i] // whole), surplus)
            holding[i] = holding[i] + extra
            surplus = surplus - extra
    return np.array(holding)


def normal_values(own_key, shape, spread, reach, pieces=(), kind=jnp.bfloat16):
    gain = levels(own_key, shape, pieces, -0.22, 0.18) if pieces else 1.0
    entries = jax.random.normal(own_key, shape, jnp.float32) * spread * gain
    return jnp.minimum(jnp.maximum(entries, -reach), reach).astype(kind)


def setup_inputs(seed: int = 0) -> dict:
    streams_of = jax.random.split(jax.random.key(seed), 10)
    tokens = normal_values(streams_of[0], (TOKENS, D), 1.0, 6.0, ((0, 64),))
    expert_ids_keys = jax.random.split(jax.random.fold_in(streams_of[1], 1), TOKENS // TOK_DEV)
    expert_ids_turns = jax.random.permutation(jax.random.fold_in(streams_of[1], 3), TOKENS // TOK_DEV)
    expert_ids = jax.vmap(lambda own, number: routed_block(jax.random.fold_in(streams_of[1], 2), own, number, TOK_DEV, EXPERTS, TOPK, CAP, 2))(expert_ids_keys, expert_ids_turns).reshape((TOKENS, TOPK))
    gate_values = jnp.clip(jnp.exp(math.log(1.0) - 2.9957323 * jax.random.uniform(streams_of[2], (TOKENS, TOPK), jnp.float32) ** levels(streams_of[2], (TOKENS, TOPK), ((0, 64),), -0.2, 0.2)), 0.05, 1.0)
    w_gate = normal_values(streams_of[3], (EXPERTS, D, FE), D ** -0.5, 0.09375, ((0, 64), (2, 2)))
    w_up = normal_values(streams_of[4], (EXPERTS, D, FE), D ** -0.5, 0.09375, ((0, 64), (2, 2)))
    w_down = normal_values(streams_of[5], (EXPERTS, FE, D), FE ** -0.5, 0.1875, ((0, 64), (1, 2)))
    shared_gate = normal_values(streams_of[6], (D, FS), D ** -0.5, 0.09375, ((1, 2),))
    shared_up = normal_values(streams_of[7], (D, FS), D ** -0.5, 0.09375, ((1, 2),))
    shared_down = normal_values(streams_of[8], (FS, D), FS ** -0.5, 0.1875, ((0, 2),))
    return {"tokens": tokens, "expert_ids": expert_ids, "gate_values": gate_values, "w_gate": w_gate, "w_up": w_up, "w_down": w_down, "shared_gate": shared_gate, "shared_up": shared_up, "shared_down": shared_down}


route_scale = 2.827


def expert_apply(inputs, gate_matrix, up_matrix, down_matrix):
    gate_out = jnp.dot(inputs, gate_matrix, preferred_element_type=jnp.float32)
    up_out = jnp.dot(inputs, up_matrix, preferred_element_type=jnp.float32)
    hidden = (jax.nn.silu(gate_out) * up_out).astype(jnp.bfloat16)
    return jnp.dot(hidden, down_matrix, preferred_element_type=jnp.float32)


def reference(tokens, expert_ids, gate_values, w_gate, w_up, w_down, shared_gate, shared_up, shared_down):
    weights = route_scale * gate_values / jnp.sum(gate_values, axis=1, keepdims=True)
    flat_ids = expert_ids.reshape(-1)
    flat_weights = jnp.concatenate([weights.reshape(-1), jnp.zeros((1,), jnp.float32)])
    padded = jnp.concatenate([tokens, jnp.zeros((1, D), jnp.bfloat16)], axis=0)
    row_limit = N_EP * CAP

    def add_expert(totals, inputs):
        gate_matrix, up_matrix, down_matrix, expert = inputs
        positions = jnp.nonzero(flat_ids == expert, size=row_limit, fill_value=TOKENS * TOPK)[0].astype(jnp.int32)
        token_idx = (positions // TOPK).astype(jnp.int32)
        result = expert_apply(padded[token_idx], gate_matrix, up_matrix, down_matrix)
        result = result * flat_weights[positions][:, None]
        return totals.at[token_idx].add(result, mode="drop"), None

    start = jnp.zeros((TOKENS, D), jnp.float32)
    routed, _ = lax.scan(add_expert, start, (w_gate, w_up, w_down, jnp.arange(EXPERTS, dtype=jnp.int32)))
    shared = expert_apply(tokens, shared_gate, shared_up, shared_down)
    return (routed + shared).astype(jnp.bfloat16)
```

```python
import functools

import jax
import jax.numpy as jnp
from jax import lax
from jax.experimental import pallas as pl
from jax.experimental.pallas import tpu as pltpu
from jax.sharding import PartitionSpec as P


route_scale = 2.827
TILE = 8
F32 = jnp.float32
BF16 = jnp.bfloat16
NT = (((1,), (1,)), ((), ()))


def named(ids, experts):
    rows, top = ids.shape
    column = lax.broadcasted_iota(jnp.int32, (rows, experts), 1)
    return column, [(ids[:, k : k + 1] == column).astype(F32) for k in range(top)]


def ranks(ids, experts):
    rows = ids.shape[0]
    _, hits = named(ids, experts)
    chosen = functools.reduce(jnp.add, hits)
    row = lax.broadcasted_iota(jnp.int32, (rows, rows), 0)
    col = lax.broadcasted_iota(jnp.int32, (rows, rows), 1)
    before = (col < row).astype(F32).astype(BF16)
    rank = jnp.dot(before, chosen.astype(BF16), preferred_element_type=F32)
    return jnp.where(chosen > 0, rank, -1.0), hits


def pick_rows(ids, experts, first):
    rank, _ = ranks(ids, experts)
    count = experts * TILE
    slot = lax.broadcasted_iota(jnp.int32, (count, experts), 0)
    expert = lax.broadcasted_iota(jnp.int32, (count, experts), 1)
    spread = (lax.shift_right_logical(slot, 3) == expert).astype(F32).astype(BF16)
    wide = lax.dot_general(spread, rank.astype(BF16), NT, preferred_element_type=F32)
    place = lax.broadcasted_iota(jnp.int32, wide.shape, 0) & (TILE - 1)
    return (wide == (place + first).astype(F32)).astype(F32).astype(BF16)


def weigh_rows(ids, gates, experts, first):
    rank, hits = ranks(ids, experts)
    weights = route_scale * gates / jnp.sum(gates, axis=1, keepdims=True)
    by_expert = functools.reduce(
        jnp.add, [hit * weights[:, k : k + 1] for k, hit in enumerate(hits)]
    )
    count = experts * TILE
    expert = lax.broadcasted_iota(jnp.int32, (experts, count), 0)
    slot = lax.broadcasted_iota(jnp.int32, (experts, count), 1)
    spread = (lax.shift_right_logical(slot, 3) == expert).astype(F32).astype(BF16)
    wide = jnp.dot(rank.astype(BF16), spread, preferred_element_type=F32)
    place = lax.broadcasted_iota(jnp.int32, wide.shape, 1) & (TILE - 1)
    here = wide == (place + first).astype(F32)
    high = by_expert.astype(BF16)
    low = (by_expert - high.astype(F32)).astype(BF16)
    parts = [
        jnp.where(here, jnp.dot(part, spread, preferred_element_type=F32), 0.0).astype(BF16)
        for part in (high, low)
    ]
    return jnp.concatenate(parts, axis=0)


def dispatch_body(experts, tail, core, ids, tokens, out, picks):
    @pl.when(pl.program_id(0) == 0)
    def _():
        first = 2 * TILE if tail else core[0] * TILE
        picks[...] = pick_rows(ids[...], experts, first)

    out[...] = jnp.dot(picks[...], tokens[...], preferred_element_type=F32).astype(BF16)


def dispatch(core, ids, tokens, experts, tail):
    rows, width = tokens.shape
    block = width // 4
    steps = 2 if tail else 4
    column = (lambda i, c: (0, 2 * c[0] + i)) if tail else (lambda i, c: (0, i))
    return pl.pallas_call(
        functools.partial(dispatch_body, experts, tail),
        out_shape=jax.ShapeDtypeStruct((experts * TILE, steps * block), BF16),
        grid_spec=pltpu.PrefetchScalarGridSpec(
            num_scalar_prefetch=1,
            grid=(steps,),
            in_specs=[
                pl.BlockSpec(ids.shape, lambda i, c: (0, 0)),
                pl.BlockSpec((rows, block), column),
            ],
            out_specs=pl.BlockSpec((experts * TILE, block), lambda i, c: (0, i)),
            scratch_shapes=[pltpu.VMEM((experts * TILE, rows), BF16)],
        ),
        name="dispatch_tail" if tail else "dispatch_head",
    )(core, ids, tokens)


def tables_body(experts, core, ids, gates, head, tail):
    head[...] = weigh_rows(ids[...], gates[...], experts, core[0] * TILE)
    tail[...] = weigh_rows(ids[...], gates[...], experts, 2 * TILE)


def tables(core, ids, gates, experts):
    shape = jax.ShapeDtypeStruct((2 * ids.shape[0], experts * TILE), BF16)
    whole = lambda s: pl.BlockSpec(s, lambda i, c: (0, 0))
    return pl.pallas_call(
        functools.partial(tables_body, experts),
        out_shape=(shape, shape),
        grid_spec=pltpu.PrefetchScalarGridSpec(
            num_scalar_prefetch=1,
            grid=(1,),
            in_specs=[whole(ids.shape), whole(gates.shape)],
            out_specs=(whole(shape.shape), whole(shape.shape)),
        ),
        name="weight_tables",
    )(core, ids, gates)


def expert_steps(core, steps, xs, own, other, total):
    step = pl.program_id(0)

    def add(g, u, d):
        gate_out = up_out = None
        for p, x in enumerate(xs):
            width = x.shape[1]
            where = p + core - 2 * p * core
            span = slice(None) if len(xs) == 1 else pl.ds(pl.multiple_of(where * width, 128), width)
            a = jnp.dot(x[...], g[span, :], preferred_element_type=F32)
            b = jnp.dot(x[...], u[span, :], preferred_element_type=F32)
            gate_out = a if gate_out is None else gate_out + a
            up_out = b if up_out is None else up_out + b
        hidden = (gate_out / (1.0 + jnp.exp(-gate_out)) * up_out).astype(BF16)
        return jnp.dot(hidden, d[...], preferred_element_type=F32)

    @pl.when(step == 0)
    def _():
        total[...] = add(*own)

    @pl.when((step > 0) & (step < steps))
    def _():
        total[...] += add(*own)

    @pl.when(step >= steps)
    def _():
        total[...] += add(*other)

    return step == 2 * steps - 1


def head_body(steps, core, x, g0, u0, d0, g1, u1, d1, out, total):
    last = expert_steps(core[0], steps, (x,), (g0, u0, d0), (g1, u1, d1), total)

    @pl.when(last)
    def _():
        out[...] = total[...].astype(BF16)


def tail_body(steps, core, x0, x1, g0, u0, d0, g1, u1, d1, keep, send, total):
    last = expert_steps(core[0], steps, (x0, x1), (g0, u0, d0), (g1, u1, d1), total)

    @pl.when(last)
    def _():
        width = keep.shape[1]
        mine = pl.multiple_of(core[0] * width, 128)
        theirs = pl.multiple_of((1 - core[0]) * width, 128)
        keep[...] = total[:, pl.ds(mine, width)].astype(BF16)
        send[...] = total[:, pl.ds(theirs, width)].astype(BF16)


def expert_apply(core, xs, own, other):
    rows = xs[0].shape[-2]
    width, hidden = own[0].shape
    block = 256
    steps = hidden // block
    first = lambda i: jnp.minimum(i, steps - 1)
    second = lambda i: jnp.maximum(i - steps, 0)
    specs = []
    for pick in (first, second):
        specs += [pl.BlockSpec((width, block), lambda i, c, pick=pick: (0, pick(i)))] * 2
        specs += [pl.BlockSpec((block, width), lambda i, c, pick=pick: (pick(i), 0))]
    once = pl.Buffered(1)
    whole = lambda s: pl.BlockSpec(s, lambda i, c: (0, 0), pipeline_mode=once)
    if len(xs) == 1:
        x_specs = [whole(xs[0].shape)]
        out = jax.ShapeDtypeStruct((rows, width), BF16)
        body, out_specs = head_body, whole(out.shape)
    else:
        half = width // 2
        mine = pl.BlockSpec((pl.Squeezed(), rows, half), lambda i, c: (c[0], 0, 0), pipeline_mode=once)
        x_specs = [mine, whole((rows, half))]
        out = (jax.ShapeDtypeStruct((rows, half), BF16),) * 2
        body, out_specs = tail_body, (whole((rows, half)),) * 2
    return pl.pallas_call(
        functools.partial(body, steps),
        out_shape=out,
        grid_spec=pltpu.PrefetchScalarGridSpec(
            num_scalar_prefetch=1,
            grid=(2 * steps,),
            in_specs=x_specs + specs,
            out_specs=out_specs,
            scratch_shapes=[pltpu.VMEM((rows, width), F32)],
        ),
        cost_estimate=pl.CostEstimate(
            flops=12 * rows * width * hidden,
            transcendentals=2 * rows * hidden,
            bytes_accessed=4 * rows * width + 12 * width * hidden,
        ),
        compiler_params=pltpu.CompilerParams(vmem_limit_bytes=56 << 20),
    )(core, *xs, *own, *other)


def weighted(table, rows):
    both = jnp.dot(table, rows, preferred_element_type=F32)
    half = both.shape[0] // 2
    return both[:half] + both[half:]


def combine_head_body(core, table, rows, shared, send, keep):
    value = weighted(table[...], rows[...]) + shared[...]

    @pl.when(pl.program_id(0) < 2)
    def _():
        send[...] = value

    @pl.when(pl.program_id(0) >= 2)
    def _():
        keep[...] = value


def combine_head(core, table, rows, shared):
    count, width = rows.shape
    tokens = shared.shape[0]
    block = width // 4
    column = lambda i, c: (0, jnp.where(i < 2, 2 * (1 - c[0]) + i, 2 * c[0] + i - 2))
    out = jax.ShapeDtypeStruct((tokens, 2 * block), F32)
    return pl.pallas_call(
        combine_head_body,
        out_shape=(out, out),
        grid_spec=pltpu.PrefetchScalarGridSpec(
            num_scalar_prefetch=1,
            grid=(4,),
            in_specs=[
                pl.BlockSpec(table.shape, lambda i, c: (0, 0)),
                pl.BlockSpec((count, block), column),
                pl.BlockSpec((tokens, block), column),
            ],
            out_specs=(
                pl.BlockSpec((tokens, block), lambda i, c: (0, jnp.minimum(i, 1))),
                pl.BlockSpec((tokens, block), lambda i, c: (0, jnp.maximum(i - 2, 0))),
            ),
        ),
        name="combine_head",
    )(core, table, rows, shared)


def combine_tail_body(table, rows, keep, received, out):
    value = weighted(table[...], rows[...]) + (keep[...] + received[...])
    out[...] = value.astype(BF16)


def combine_tail(table, rows, keep, received):
    count, width = rows.shape
    tokens = keep.shape[0]
    block = width // 2
    return pl.pallas_call(
        combine_tail_body,
        out_shape=jax.ShapeDtypeStruct((tokens, width), BF16),
        grid=(2,),
        in_specs=[
            pl.BlockSpec(table.shape, lambda i: (0, 0)),
            pl.BlockSpec((count, block), lambda i: (0, i)),
            pl.BlockSpec((tokens, block), lambda i: (0, i)),
            pl.BlockSpec((tokens, block), lambda i: (0, i)),
        ],
        out_specs=pl.BlockSpec((tokens, block), lambda i: (0, i)),
        name="combine_tail",
    )(table, rows, keep, received)


def shared_apply(inputs, gate_matrix, up_matrix, down_matrix):
    gate_out = jnp.dot(inputs, gate_matrix, preferred_element_type=F32)
    up_out = jnp.dot(inputs, up_matrix, preferred_element_type=F32)
    hidden = (jax.nn.silu(gate_out) * up_out).astype(BF16)
    return jnp.dot(hidden, down_matrix, preferred_element_type=F32)


def exchange(x, axis):
    return lax.all_to_all(x, axis, split_axis=0, concat_axis=0, tiled=True)


def per_device(
    tokens, expert_ids, gate_values, w_gate, w_up, w_down, shared_gate, shared_up, shared_down
):
    experts = lax.axis_size("ep") * w_gate.shape[0]
    width = tokens.shape[1]
    half = width // 2
    core = lax.axis_index("tp").astype(jnp.int32).reshape(1)
    swap = [(0, 1), (1, 0)]
    own = (w_gate[0], w_up[0], w_down[0])
    other = tuple(lax.ppermute(w, "tp", swap) for w in own)
    head = dispatch(core, expert_ids, tokens, experts, False)
    head_in = exchange(head.reshape(experts, TILE, width), "ep")
    tail = dispatch(core, expert_ids, tokens, experts, True)
    tail_in = exchange(tail.reshape(experts, TILE, half), "ep")
    table_head, table_tail = tables(core, expert_ids, gate_values, experts)
    shared = shared_apply(tokens, shared_gate, shared_up, shared_down)
    head_out = expert_apply(core, (head_in.reshape(experts * TILE, width),), own, other)
    head_back = exchange(head_out.reshape(experts, TILE, width), "ep")
    tail_x = tail_in.reshape(2, experts * TILE // 2, half)
    theirs = lax.dynamic_index_in_dim(tail_x, 1 - core[0], 0, keepdims=False)
    theirs = lax.ppermute(theirs, "tp", swap)
    kept, sent = expert_apply(core, (tail_x, theirs), own, other)
    taken = lax.ppermute(sent, "tp", swap)
    tail_y = jnp.where(core[0] == 0, jnp.stack([kept, taken]), jnp.stack([taken, kept]))
    tail_back = exchange(tail_y.reshape(experts, TILE, half), "ep")
    send, keep = combine_head(core, table_head, head_back.reshape(-1, width), shared)
    received = lax.ppermute(send, "tp", swap)
    return combine_tail(table_tail, tail_back.reshape(-1, half), keep, received)


def solution(mesh):
    return jax.shard_map(
        per_device,
        mesh=mesh,
        in_specs=(
            P("ep", None),
            P("ep", None),
            P("ep", None),
            P("ep", None, "tp"),
            P("ep", None, "tp"),
            P("ep", "tp", None),
            P(None, "tp"),
            P(None, "tp"),
            P("tp", None),
        ),
        out_specs=P("ep", "tp"),
        check_vma=False,
    )
```

```python
import functools

import jax
import jax.numpy as jnp
from jax import lax
from jax.experimental import pallas as pl
from jax.experimental.pallas import tpu as pltpu
from jax.sharding import PartitionSpec as P


route_scale = 2.827
TILE = 8
F32 = jnp.float32
BF16 = jnp.bfloat16


def named(ids, experts):
    rows, top = ids.shape
    column = lax.broadcasted_iota(jnp.int32, (rows, experts), 1)
    return column, [(ids[:, k : k + 1] == column).astype(F32) for k in range(top)]


def ranks(ids, experts):
    rows = ids.shape[0]
    _, hits = named(ids, experts)
    chosen = functools.reduce(jnp.add, hits)
    row = lax.broadcasted_iota(jnp.int32, (rows, rows), 0)
    col = lax.broadcasted_iota(jnp.int32, (rows, rows), 1)
    before = (col < row).astype(F32).astype(BF16)
    rank = jnp.dot(before, chosen.astype(BF16), preferred_element_type=F32)
    return jnp.where(chosen > 0, rank, -1.0), hits


def pick_rows(ids, experts, first):
    top, rows = ids.shape
    row = lax.broadcasted_iota(jnp.int32, (experts, rows), 0)
    hits = [(ids[k : k + 1, :] == row).astype(F32) for k in range(top)]
    chosen = functools.reduce(jnp.add, hits)
    earlier = lax.broadcasted_iota(jnp.int32, (rows, rows), 0)
    later = lax.broadcasted_iota(jnp.int32, (rows, rows), 1)
    before = (earlier < later).astype(F32).astype(BF16)
    rank = jnp.dot(chosen.astype(BF16), before, preferred_element_type=F32)
    rank = jnp.where(chosen > 0, rank, -1.0)
    count = experts * TILE
    slot = lax.broadcasted_iota(jnp.int32, (count, experts), 0)
    expert = lax.broadcasted_iota(jnp.int32, (count, experts), 1)
    spread = (lax.shift_right_logical(slot, 3) == expert).astype(F32).astype(BF16)
    wide = jnp.dot(spread, rank.astype(BF16), preferred_element_type=F32)
    place = lax.broadcasted_iota(jnp.int32, wide.shape, 0) & (TILE - 1)
    return (wide == (place + first).astype(F32)).astype(F32).astype(BF16)


def weigh_rows(ids, gates, experts, first):
    rank, hits = ranks(ids, experts)
    weights = route_scale * gates / jnp.sum(gates, axis=1, keepdims=True)
    by_expert = functools.reduce(
        jnp.add, [hit * weights[:, k : k + 1] for k, hit in enumerate(hits)]
    )
    count = experts * TILE
    expert = lax.broadcasted_iota(jnp.int32, (experts, count), 0)
    slot = lax.broadcasted_iota(jnp.int32, (experts, count), 1)
    spread = (lax.shift_right_logical(slot, 3) == expert).astype(F32).astype(BF16)
    wide = jnp.dot(rank.astype(BF16), spread, preferred_element_type=F32)
    place = lax.broadcasted_iota(jnp.int32, wide.shape, 1) & (TILE - 1)
    here = wide == (place + first).astype(F32)
    high = by_expert.astype(BF16)
    low = (by_expert - high.astype(F32)).astype(BF16)
    parts = [
        jnp.where(here, jnp.dot(part, spread, preferred_element_type=F32), 0.0).astype(BF16)
        for part in (high, low)
    ]
    return jnp.concatenate(parts, axis=0)


VMEM = pl.BlockSpec(memory_space=pltpu.VMEM)
SMEM = pl.BlockSpec(memory_space=pltpu.SMEM)


HBM = pl.BlockSpec(memory_space=pl.ANY)
CHUNKS = 4


def dispatch_head_body(experts, core, ids, tokens, out, source, rows, loads, stores):
    block = source.shape[2]
    span = lambda j: pl.ds(j * block, block)
    fetch = [
        pltpu.make_async_copy(tokens.at[:, span(j)], source.at[j], loads.at[j])
        for j in range(CHUNKS)
    ]
    write = [
        pltpu.make_async_copy(rows.at[j], out.at[:, span(j)], stores.at[j]) for j in range(CHUNKS)
    ]
    for copy in fetch:
        copy.start()
    picks = pick_rows(ids[...], experts, core[0] * TILE)
    for j in range(CHUNKS):
        fetch[j].wait()
        rows[j] = jnp.dot(picks, source[j], preferred_element_type=F32).astype(BF16)
        write[j].start()
    for copy in write:
        copy.wait()


def dispatch_head(core, ids, tokens, experts):
    count, width = tokens.shape
    block = width // CHUNKS
    return pl.pallas_call(
        functools.partial(dispatch_head_body, experts),
        out_shape=jax.ShapeDtypeStruct((experts * TILE, width), BF16),
        in_specs=[SMEM, VMEM, HBM],
        out_specs=HBM,
        scratch_shapes=[
            pltpu.VMEM((CHUNKS, count, block), BF16),
            pltpu.VMEM((CHUNKS, experts * TILE, block), BF16),
            pltpu.SemaphoreType.DMA((CHUNKS,)),
            pltpu.SemaphoreType.DMA((CHUNKS,)),
        ],
        name="dispatch_head",
    )(core, ids, tokens)


def dispatch_tail_body(experts, core, ids, tokens, out, picks):
    @pl.when(pl.program_id(0) == 0)
    def _():
        picks[...] = pick_rows(ids[...], experts, 2 * TILE)

    out[...] = jnp.dot(picks[...], tokens[...], preferred_element_type=F32).astype(BF16)


def dispatch_tail(core, ids, tokens, experts):
    rows, width = tokens.shape
    block = width // 4
    return pl.pallas_call(
        functools.partial(dispatch_tail_body, experts),
        out_shape=jax.ShapeDtypeStruct((experts * TILE, 2 * block), BF16),
        grid_spec=pltpu.PrefetchScalarGridSpec(
            num_scalar_prefetch=1,
            grid=(2,),
            in_specs=[
                pl.BlockSpec(ids.shape, lambda i, c: (0, 0)),
                pl.BlockSpec((rows, block), lambda i, c: (0, 2 * c[0] + i)),
            ],
            out_specs=pl.BlockSpec((experts * TILE, block), lambda i, c: (0, i)),
            scratch_shapes=[pltpu.VMEM((experts * TILE, rows), BF16)],
        ),
        name="dispatch_tail",
    )(core, ids, tokens)


def tables_body(experts, core, ids, gates, head, tail):
    head[...] = weigh_rows(ids[...], gates[...], experts, core[0] * TILE)
    tail[...] = weigh_rows(ids[...], gates[...], experts, 2 * TILE)


def tables(core, ids, gates, experts):
    shape = jax.ShapeDtypeStruct((2 * ids.shape[0], experts * TILE), BF16)
    whole = lambda s: pl.BlockSpec(s, lambda i, c: (0, 0))
    return pl.pallas_call(
        functools.partial(tables_body, experts),
        out_shape=(shape, shape),
        grid_spec=pltpu.PrefetchScalarGridSpec(
            num_scalar_prefetch=1,
            grid=(1,),
            in_specs=[whole(ids.shape), whole(gates.shape)],
            out_specs=(whole(shape.shape), whole(shape.shape)),
        ),
        name="weight_tables",
    )(core, ids, gates)


def expert_steps(core, steps, xs, own, other, total):
    step = pl.program_id(0)

    def add(g, u, d):
        gate_out = up_out = None
        for p, x in enumerate(xs):
            width = x.shape[1]
            where = p + core - 2 * p * core
            span = slice(None) if len(xs) == 1 else pl.ds(pl.multiple_of(where * width, 128), width)
            a = jnp.dot(x[...], g[span, :], preferred_element_type=F32)
            b = jnp.dot(x[...], u[span, :], preferred_element_type=F32)
            gate_out = a if gate_out is None else gate_out + a
            up_out = b if up_out is None else up_out + b
        hidden = (gate_out / (1.0 + jnp.exp(-gate_out)) * up_out).astype(BF16)
        return jnp.dot(hidden, d[...], preferred_element_type=F32)

    @pl.when(step == 0)
    def _():
        total[...] = add(*own)

    @pl.when((step > 0) & (step < steps))
    def _():
        total[...] += add(*own)

    @pl.when(step >= steps)
    def _():
        total[...] += add(*other)

    return step == 2 * steps - 1


def head_body(steps, core, x, g0, u0, d0, g1, u1, d1, out, total):
    last = expert_steps(core[0], steps, (x,), (g0, u0, d0), (g1, u1, d1), total)

    @pl.when(last)
    def _():
        out[...] = total[...].astype(BF16)


def tail_body(steps, core, x0, x1, g0, u0, d0, g1, u1, d1, keep, send, total):
    last = expert_steps(core[0], steps, (x0, x1), (g0, u0, d0), (g1, u1, d1), total)

    @pl.when(last)
    def _():
        width = keep.shape[1]
        mine = pl.multiple_of(core[0] * width, 128)
        theirs = pl.multiple_of((1 - core[0]) * width, 128)
        keep[...] = total[:, pl.ds(mine, width)].astype(BF16)
        send[...] = total[:, pl.ds(theirs, width)].astype(BF16)


def expert_apply(core, xs, own, other):
    rows = xs[0].shape[-2]
    width, hidden = own[0].shape
    block = 256
    steps = hidden // block
    first = lambda i: jnp.minimum(i, steps - 1)
    second = lambda i: jnp.maximum(i - steps, 0)
    specs = []
    for pick in (first, second):
        specs += [pl.BlockSpec((width, block), lambda i, c, pick=pick: (0, pick(i)))] * 2
        specs += [pl.BlockSpec((block, width), lambda i, c, pick=pick: (pick(i), 0))]
    once = pl.Buffered(1)
    whole = lambda s: pl.BlockSpec(s, lambda i, c: (0, 0), pipeline_mode=once)
    if len(xs) == 1:
        x_specs = [whole(xs[0].shape)]
        out = jax.ShapeDtypeStruct((rows, width), BF16)
        body, out_specs = head_body, whole(out.shape)
    else:
        half = width // 2
        mine = pl.BlockSpec((pl.Squeezed(), rows, half), lambda i, c: (c[0], 0, 0), pipeline_mode=once)
        x_specs = [mine, whole((rows, half))]
        out = (jax.ShapeDtypeStruct((rows, half), BF16),) * 2
        body, out_specs = tail_body, (whole((rows, half)),) * 2
    return pl.pallas_call(
        functools.partial(body, steps),
        out_shape=out,
        grid_spec=pltpu.PrefetchScalarGridSpec(
            num_scalar_prefetch=1,
            grid=(2 * steps,),
            in_specs=x_specs + specs,
            out_specs=out_specs,
            scratch_shapes=[pltpu.VMEM((rows, width), F32)],
        ),
        cost_estimate=pl.CostEstimate(
            flops=12 * rows * width * hidden,
            transcendentals=2 * rows * hidden,
            bytes_accessed=4 * rows * width + 12 * width * hidden,
        ),
        compiler_params=pltpu.CompilerParams(vmem_limit_bytes=56 << 20),
    )(core, *xs, *own, *other)


def weighted(table, rows):
    both = jnp.dot(table, rows, preferred_element_type=F32)
    half = both.shape[0] // 2
    return both[:half] + both[half:]


def combine_head_body(core, table, rows, shared, send, keep):
    value = weighted(table[...], rows[...]) + shared[...]

    @pl.when(pl.program_id(0) < 2)
    def _():
        send[...] = value

    @pl.when(pl.program_id(0) >= 2)
    def _():
        keep[...] = value


def combine_head(core, table, rows, shared):
    count, width = rows.shape
    tokens = shared.shape[0]
    block = width // 4
    column = lambda i, c: (0, jnp.where(i < 2, 2 * (1 - c[0]) + i, 2 * c[0] + i - 2))
    out = jax.ShapeDtypeStruct((tokens, 2 * block), F32)
    return pl.pallas_call(
        combine_head_body,
        out_shape=(out, out),
        grid_spec=pltpu.PrefetchScalarGridSpec(
            num_scalar_prefetch=1,
            grid=(4,),
            in_specs=[
                pl.BlockSpec(table.shape, lambda i, c: (0, 0)),
                pl.BlockSpec((count, block), column),
                pl.BlockSpec((tokens, block), column),
            ],
            out_specs=(
                pl.BlockSpec((tokens, block), lambda i, c: (0, jnp.minimum(i, 1))),
                pl.BlockSpec((tokens, block), lambda i, c: (0, jnp.maximum(i - 2, 0))),
            ),
        ),
        compiler_params=pltpu.CompilerParams(vmem_limit_bytes=24 << 20),
        name="combine_head",
    )(core, table, rows, shared)


def combine_tail_body(table, rows, keep, received, out):
    value = weighted(table[...], rows[...]) + (keep[...] + received[...])
    out[...] = value.astype(BF16)


def combine_tail(table, rows, keep, received):
    return pl.pallas_call(
        combine_tail_body,
        out_shape=jax.ShapeDtypeStruct(keep.shape, BF16),
        in_specs=[VMEM] * 4,
        out_specs=VMEM,
        compiler_params=pltpu.CompilerParams(vmem_limit_bytes=24 << 20),
        name="combine_tail",
    )(*[pltpu.with_memory_space_constraint(v, pltpu.VMEM) for v in (table, rows, keep, received)])


def shared_apply(inputs, gate_matrix, up_matrix, down_matrix):
    gate_out = jnp.dot(inputs, gate_matrix, preferred_element_type=F32)
    up_out = jnp.dot(inputs, up_matrix, preferred_element_type=F32)
    hidden = (jax.nn.silu(gate_out) * up_out).astype(BF16)
    return jnp.dot(hidden, down_matrix, preferred_element_type=F32)


def exchange(x, axis):
    return lax.all_to_all(x, axis, split_axis=0, concat_axis=0, tiled=True)


def per_device(
    tokens, expert_ids, gate_values, w_gate, w_up, w_down, shared_gate, shared_up, shared_down
):
    experts = lax.axis_size("ep") * w_gate.shape[0]
    width = tokens.shape[1]
    half = width // 2
    core = lax.axis_index("tp").astype(jnp.int32).reshape(1)
    swap = [(0, 1), (1, 0)]
    own = (w_gate[0], w_up[0], w_down[0])
    other = tuple(lax.ppermute(w, "tp", swap) for w in own)
    ids = expert_ids.T
    head = dispatch_head(core, ids, tokens, experts)
    head_in = exchange(head.reshape(experts, TILE, width), "ep")
    tail = dispatch_tail(core, ids, tokens, experts)
    tail_in = exchange(tail.reshape(experts, TILE, half), "ep")
    table_head, table_tail = tables(core, expert_ids, gate_values, experts)
    shared = shared_apply(tokens, shared_gate, shared_up, shared_down)
    head_out = expert_apply(core, (head_in.reshape(experts * TILE, width),), own, other)
    head_back = exchange(head_out.reshape(experts, TILE, width), "ep")
    tail_x = tail_in.reshape(2, experts * TILE // 2, half)
    theirs = lax.dynamic_index_in_dim(tail_x, 1 - core[0], 0, keepdims=False)
    theirs = lax.ppermute(theirs, "tp", swap)
    kept, sent = expert_apply(core, (tail_x, theirs), own, other)
    taken = lax.ppermute(sent, "tp", swap)
    tail_y = jnp.where(core[0] == 0, jnp.stack([kept, taken]), jnp.stack([taken, kept]))
    tail_back = exchange(tail_y.reshape(experts, TILE, half), "ep")
    send, keep = combine_head(core, table_head, head_back.reshape(-1, width), shared)
    received = lax.ppermute(send, "tp", swap)
    return combine_tail(table_tail, tail_back.reshape(-1, half), keep, received)


def solution(mesh):
    return jax.shard_map(
        per_device,
        mesh=mesh,
        in_specs=(
            P("ep", None),
            P("ep", None),
            P("ep", None),
            P("ep", None, "tp"),
            P("ep", None, "tp"),
            P("ep", "tp", None),
            P(None, "tp"),
            P(None, "tp"),
            P("tp", None),
        ),
        out_specs=P("ep", "tp"),
        check_vma=False,
    )
```

```python
import functools

import jax
import jax.numpy as jnp
from jax import lax
from jax.experimental import pallas as pl
from jax.experimental.pallas import tpu as pltpu
from jax.sharding import PartitionSpec as P


route_scale = 2.827
TILE = 8
F32 = jnp.float32
BF16 = jnp.bfloat16


def named(ids, experts):
    rows, top = ids.shape
    column = lax.broadcasted_iota(jnp.int32, (rows, experts), 1)
    return column, [(ids[:, k : k + 1] == column).astype(F32) for k in range(top)]


def ranks(ids, experts):
    rows = ids.shape[0]
    _, hits = named(ids, experts)
    chosen = functools.reduce(jnp.add, hits)
    row = lax.broadcasted_iota(jnp.int32, (rows, rows), 0)
    col = lax.broadcasted_iota(jnp.int32, (rows, rows), 1)
    before = (col < row).astype(F32).astype(BF16)
    rank = jnp.dot(before, chosen.astype(BF16), preferred_element_type=F32)
    return jnp.where(chosen > 0, rank, -1.0), hits


def pick_rows(ids, experts, first):
    top, rows = ids.shape
    row = lax.broadcasted_iota(jnp.int32, (experts, rows), 0)
    hits = [(ids[k : k + 1, :] == row).astype(F32) for k in range(top)]
    chosen = functools.reduce(jnp.add, hits)
    earlier = lax.broadcasted_iota(jnp.int32, (rows, rows), 0)
    later = lax.broadcasted_iota(jnp.int32, (rows, rows), 1)
    before = (earlier < later).astype(F32).astype(BF16)
    rank = jnp.dot(chosen.astype(BF16), before, preferred_element_type=F32)
    rank = jnp.where(chosen > 0, rank, -1.0)
    count = experts * TILE
    slot = lax.broadcasted_iota(jnp.int32, (count, experts), 0)
    expert = lax.broadcasted_iota(jnp.int32, (count, experts), 1)
    spread = (lax.shift_right_logical(slot, 3) == expert).astype(F32).astype(BF16)
    wide = jnp.dot(spread, rank.astype(BF16), preferred_element_type=F32)
    place = lax.broadcasted_iota(jnp.int32, wide.shape, 0) & (TILE - 1)
    return (wide == (place + first).astype(F32)).astype(F32).astype(BF16)


def weigh_rows(ids, gates, experts, first):
    rank, hits = ranks(ids, experts)
    weights = route_scale * gates / jnp.sum(gates, axis=1, keepdims=True)
    by_expert = functools.reduce(
        jnp.add, [hit * weights[:, k : k + 1] for k, hit in enumerate(hits)]
    )
    count = experts * TILE
    expert = lax.broadcasted_iota(jnp.int32, (experts, count), 0)
    slot = lax.broadcasted_iota(jnp.int32, (experts, count), 1)
    spread = (lax.shift_right_logical(slot, 3) == expert).astype(F32).astype(BF16)
    wide = jnp.dot(rank.astype(BF16), spread, preferred_element_type=F32)
    place = lax.broadcasted_iota(jnp.int32, wide.shape, 1) & (TILE - 1)
    here = wide == (place + first).astype(F32)
    high = by_expert.astype(BF16)
    low = (by_expert - high.astype(F32)).astype(BF16)
    parts = [
        jnp.where(here, jnp.dot(part, spread, preferred_element_type=F32), 0.0).astype(BF16)
        for part in (high, low)
    ]
    return jnp.concatenate(parts, axis=0)


VMEM = pl.BlockSpec(memory_space=pltpu.VMEM)
SMEM = pl.BlockSpec(memory_space=pltpu.SMEM)


HBM = pl.BlockSpec(memory_space=pl.ANY)
CHUNKS = 7


def dispatch_head_body(experts, core, ids, tokens, out, source, rows, loads, stores):
    block = source.shape[2]
    span = lambda j: pl.ds(j * block, block)
    fetch = [
        pltpu.make_async_copy(tokens.at[:, span(j)], source.at[j], loads.at[j])
        for j in range(CHUNKS)
    ]
    write = [
        pltpu.make_async_copy(rows.at[j], out.at[:, span(j)], stores.at[j]) for j in range(CHUNKS)
    ]
    for copy in fetch:
        copy.start()
    picks = pick_rows(ids[...], experts, core[0] * TILE)
    for j in range(CHUNKS):
        fetch[j].wait()
        rows[j] = jnp.dot(picks, source[j], preferred_element_type=F32).astype(BF16)
        write[j].start()
    for copy in write:
        copy.wait()


def dispatch_head(core, ids, tokens, experts):
    count, width = tokens.shape
    block = width // CHUNKS
    return pl.pallas_call(
        functools.partial(dispatch_head_body, experts),
        out_shape=jax.ShapeDtypeStruct((experts * TILE, width), BF16),
        in_specs=[SMEM, VMEM, HBM],
        out_specs=HBM,
        scratch_shapes=[
            pltpu.VMEM((CHUNKS, count, block), BF16),
            pltpu.VMEM((CHUNKS, experts * TILE, block), BF16),
            pltpu.SemaphoreType.DMA((CHUNKS,)),
            pltpu.SemaphoreType.DMA((CHUNKS,)),
        ],
        name="dispatch_head",
    )(core, ids, tokens)


def dispatch_tail_body(experts, core, ids, tokens, out, picks):
    @pl.when(pl.program_id(0) == 0)
    def _():
        picks[...] = pick_rows(ids[...], experts, 2 * TILE)

    out[...] = jnp.dot(picks[...], tokens[...], preferred_element_type=F32).astype(BF16)


def dispatch_tail(core, ids, tokens, experts):
    rows, width = tokens.shape
    block = width // 4
    return pl.pallas_call(
        functools.partial(dispatch_tail_body, experts),
        out_shape=jax.ShapeDtypeStruct((experts * TILE, 2 * block), BF16),
        grid_spec=pltpu.PrefetchScalarGridSpec(
            num_scalar_prefetch=1,
            grid=(2,),
            in_specs=[
                pl.BlockSpec(ids.shape, lambda i, c: (0, 0)),
                pl.BlockSpec((rows, block), lambda i, c: (0, 2 * c[0] + i)),
            ],
            out_specs=pl.BlockSpec((experts * TILE, block), lambda i, c: (0, i)),
            scratch_shapes=[pltpu.VMEM((experts * TILE, rows), BF16)],
        ),
        name="dispatch_tail",
    )(core, ids, tokens)


def tables_body(experts, core, ids, gates, head, tail):
    head[...] = weigh_rows(ids[...], gates[...], experts, core[0] * TILE)
    tail[...] = weigh_rows(ids[...], gates[...], experts, 2 * TILE)


def tables(core, ids, gates, experts):
    shape = jax.ShapeDtypeStruct((2 * ids.shape[0], experts * TILE), BF16)
    whole = lambda s: pl.BlockSpec(s, lambda i, c: (0, 0))
    return pl.pallas_call(
        functools.partial(tables_body, experts),
        out_shape=(shape, shape),
        grid_spec=pltpu.PrefetchScalarGridSpec(
            num_scalar_prefetch=1,
            grid=(1,),
            in_specs=[whole(ids.shape), whole(gates.shape)],
            out_specs=(whole(shape.shape), whole(shape.shape)),
        ),
        name="weight_tables",
    )(core, ids, gates)


def expert_steps(core, steps, xs, own, other, total):
    step = pl.program_id(0)

    def add(g, u, d):
        gate_out = up_out = None
        for p, x in enumerate(xs):
            width = x.shape[1]
            where = p + core - 2 * p * core
            span = slice(None) if len(xs) == 1 else pl.ds(pl.multiple_of(where * width, 128), width)
            a = jnp.dot(x[...], g[span, :], preferred_element_type=F32)
            b = jnp.dot(x[...], u[span, :], preferred_element_type=F32)
            gate_out = a if gate_out is None else gate_out + a
            up_out = b if up_out is None else up_out + b
        hidden = (gate_out / (1.0 + jnp.exp(-gate_out)) * up_out).astype(BF16)
        return jnp.dot(hidden, d[...], preferred_element_type=F32)

    @pl.when(step == 0)
    def _():
        total[...] = add(*own)

    @pl.when((step > 0) & (step < steps))
    def _():
        total[...] += add(*own)

    @pl.when(step >= steps)
    def _():
        total[...] += add(*other)

    return step == 2 * steps - 1


def head_body(steps, core, x, g0, u0, d0, g1, u1, d1, out, total):
    last = expert_steps(core[0], steps, (x,), (g0, u0, d0), (g1, u1, d1), total)

    @pl.when(last)
    def _():
        out[...] = total[...].astype(BF16)


def tail_body(steps, core, x0, x1, g0, u0, d0, g1, u1, d1, keep, send, total):
    last = expert_steps(core[0], steps, (x0, x1), (g0, u0, d0), (g1, u1, d1), total)

    @pl.when(last)
    def _():
        width = keep.shape[1]
        mine = pl.multiple_of(core[0] * width, 128)
        theirs = pl.multiple_of((1 - core[0]) * width, 128)
        keep[...] = total[:, pl.ds(mine, width)].astype(BF16)
        send[...] = total[:, pl.ds(theirs, width)].astype(BF16)


def expert_apply(core, xs, own, other):
    rows = xs[0].shape[-2]
    width, hidden = own[0].shape
    block = 256
    steps = hidden // block
    first = lambda i: jnp.minimum(i, steps - 1)
    second = lambda i: jnp.maximum(i - steps, 0)
    specs = []
    for pick in (first, second):
        specs += [pl.BlockSpec((width, block), lambda i, c, pick=pick: (0, pick(i)))] * 2
        specs += [pl.BlockSpec((block, width), lambda i, c, pick=pick: (pick(i), 0))]
    once = pl.Buffered(1)
    whole = lambda s: pl.BlockSpec(s, lambda i, c: (0, 0), pipeline_mode=once)
    if len(xs) == 1:
        x_specs = [whole(xs[0].shape)]
        out = jax.ShapeDtypeStruct((rows, width), BF16)
        body, out_specs = head_body, whole(out.shape)
    else:
        half = width // 2
        mine = pl.BlockSpec((pl.Squeezed(), rows, half), lambda i, c: (c[0], 0, 0), pipeline_mode=once)
        x_specs = [mine, whole((rows, half))]
        out = (jax.ShapeDtypeStruct((rows, half), BF16),) * 2
        body, out_specs = tail_body, (whole((rows, half)),) * 2
    return pl.pallas_call(
        functools.partial(body, steps),
        out_shape=out,
        grid_spec=pltpu.PrefetchScalarGridSpec(
            num_scalar_prefetch=1,
            grid=(2 * steps,),
            in_specs=x_specs + specs,
            out_specs=out_specs,
            scratch_shapes=[pltpu.VMEM((rows, width), F32)],
        ),
        cost_estimate=pl.CostEstimate(
            flops=12 * rows * width * hidden,
            transcendentals=2 * rows * hidden,
            bytes_accessed=4 * rows * width + 12 * width * hidden,
        ),
        compiler_params=pltpu.CompilerParams(vmem_limit_bytes=56 << 20),
    )(core, *xs, *own, *other)


def weighted(table, rows):
    both = jnp.dot(table, rows, preferred_element_type=F32)
    half = both.shape[0] // 2
    return both[:half] + both[half:]


def combine_head_body(core, table, rows, shared, send, keep):
    value = weighted(table[...], rows[...]) + shared[...]

    @pl.when(pl.program_id(0) < 2)
    def _():
        send[...] = value

    @pl.when(pl.program_id(0) >= 2)
    def _():
        keep[...] = value


def combine_head(core, table, rows, shared):
    count, width = rows.shape
    tokens = shared.shape[0]
    block = width // 4
    column = lambda i, c: (0, jnp.where(i < 2, 2 * (1 - c[0]) + i, 2 * c[0] + i - 2))
    out = jax.ShapeDtypeStruct((tokens, 2 * block), F32)
    return pl.pallas_call(
        combine_head_body,
        out_shape=(out, out),
        grid_spec=pltpu.PrefetchScalarGridSpec(
            num_scalar_prefetch=1,
            grid=(4,),
            in_specs=[
                pl.BlockSpec(table.shape, lambda i, c: (0, 0)),
                pl.BlockSpec((count, block), column),
                pl.BlockSpec((tokens, block), column),
            ],
            out_specs=(
                pl.BlockSpec((tokens, block), lambda i, c: (0, jnp.minimum(i, 1))),
                pl.BlockSpec((tokens, block), lambda i, c: (0, jnp.maximum(i - 2, 0))),
            ),
        ),
        compiler_params=pltpu.CompilerParams(vmem_limit_bytes=24 << 20),
        name="combine_head",
    )(core, table, rows, shared)


def combine_tail_body(table, rows, keep, received, out, source, value, loads, stores):
    block = source.shape[2]
    span = lambda j: pl.ds(j * block, block)
    fetch = [
        pltpu.make_async_copy(rows.at[:, span(j)], source.at[j], loads.at[j]) for j in range(CHUNKS)
    ]
    write = [
        pltpu.make_async_copy(value.at[j], out.at[:, span(j)], stores.at[j]) for j in range(CHUNKS)
    ]
    for copy in fetch:
        copy.start()
    for j in range(CHUNKS):
        fetch[j].wait()
        total = weighted(table[...], source[j]) + (keep[:, span(j)] + received[:, span(j)])
        value[j] = total.astype(BF16)
        write[j].start()
    for copy in write:
        copy.wait()


def combine_tail(table, rows, keep, received):
    near = lambda v: pltpu.with_memory_space_constraint(v, pltpu.VMEM)
    count, width = rows.shape
    tokens = keep.shape[0]
    block = width // CHUNKS
    return pl.pallas_call(
        combine_tail_body,
        out_shape=jax.ShapeDtypeStruct(keep.shape, BF16),
        in_specs=[VMEM, HBM, VMEM, VMEM],
        out_specs=HBM,
        scratch_shapes=[
            pltpu.VMEM((CHUNKS, count, block), BF16),
            pltpu.VMEM((CHUNKS, tokens, block), BF16),
            pltpu.SemaphoreType.DMA((CHUNKS,)),
            pltpu.SemaphoreType.DMA((CHUNKS,)),
        ],
        compiler_params=pltpu.CompilerParams(vmem_limit_bytes=24 << 20),
        name="combine_tail",
    )(near(table), rows, near(keep), near(received))


def shared_apply(inputs, gate_matrix, up_matrix, down_matrix):
    gate_out = jnp.dot(inputs, gate_matrix, preferred_element_type=F32)
    up_out = jnp.dot(inputs, up_matrix, preferred_element_type=F32)
    hidden = (jax.nn.silu(gate_out) * up_out).astype(BF16)
    return jnp.dot(hidden, down_matrix, preferred_element_type=F32)


def exchange(x, axis):
    return lax.all_to_all(x, axis, split_axis=0, concat_axis=0, tiled=True)


def per_device(
    tokens, expert_ids, gate_values, w_gate, w_up, w_down, shared_gate, shared_up, shared_down
):
    experts = lax.axis_size("ep") * w_gate.shape[0]
    width = tokens.shape[1]
    half = width // 2
    core = lax.axis_index("tp").astype(jnp.int32).reshape(1)
    swap = [(0, 1), (1, 0)]
    own = (w_gate[0], w_up[0], w_down[0])
    other = tuple(lax.ppermute(w, "tp", swap) for w in own)
    ids = expert_ids.T
    head = dispatch_head(core, ids, tokens, experts)
    head_in = exchange(head.reshape(experts, TILE, width), "ep")
    tail = dispatch_tail(core, ids, tokens, experts)
    tail_in = exchange(tail.reshape(experts, TILE, half), "ep")
    table_head, table_tail = tables(core, expert_ids, gate_values, experts)
    shared = shared_apply(tokens, shared_gate, shared_up, shared_down)
    head_out = expert_apply(core, (head_in.reshape(experts * TILE, width),), own, other)
    head_back = exchange(head_out.reshape(experts, TILE, width), "ep")
    tail_x = tail_in.reshape(2, experts * TILE // 2, half)
    theirs = lax.dynamic_index_in_dim(tail_x, 1 - core[0], 0, keepdims=False)
    theirs = lax.ppermute(theirs, "tp", swap)
    kept, sent = expert_apply(core, (tail_x, theirs), own, other)
    taken = lax.ppermute(sent, "tp", swap)
    tail_y = jnp.where(core[0] == 0, jnp.stack([kept, taken]), jnp.stack([taken, kept]))
    tail_back = exchange(tail_y.reshape(experts, TILE, half), "ep")
    send, keep = combine_head(core, table_head, head_back.reshape(-1, width), shared)
    received = lax.ppermute(send, "tp", swap)
    return combine_tail(table_tail, tail_back.reshape(-1, half), keep, received)


def solution(mesh):
    return jax.shard_map(
        per_device,
        mesh=mesh,
        in_specs=(
            P("ep", None),
            P("ep", None),
            P("ep", None),
            P("ep", None, "tp"),
            P("ep", None, "tp"),
            P("ep", "tp", None),
            P(None, "tp"),
            P(None, "tp"),
            P("tp", None),
        ),
        out_specs=P("ep", "tp"),
        check_vma=False,
    )
```
